32 devices in a mesh: dp: 4 (over x, core), label: 8 (over z, y).
Axes of the slice: x: 2, y: 2, z: 4, core: 2. Of those that a mesh axis runs over, the one named last changes fastest.
Arguments:
- features: bfloat16 [8192, 768], P(('dp', 'label')), may hold values from -6 to 6
- head_targets: int32 [8192, 4], P(('dp', 'label')), may hold values from 0 to 255
- tail_labels: int32 [8192, 16], P(('dp', 'label')), may hold values from 0 to 1023, as said below
- tail_positive: int32 [8192, 16], P(('dp', 'label')), may hold values 0 or 1
- slots: int32 [32, 8, 128], P(('dp', 'label')), may hold values from 0 to 255, as said below
- counts: int32 [32, 8], P(('dp', 'label')), may hold values from 0 to 128, as said below
- head_weight: float32 [256, 768], P('label'), may hold values from -0.21875 to 0.21875
- head_first: float32 [256, 768], P('label'), may hold values from -0.03125 to 0.03125
- head_second: float32 [256, 768], P('label'), may hold values from 1e-07 to 2e-05
- tail_weight: float32 [1024, 768], P('label'), may hold values from -0.21875 to 0.21875
- tail_first: float32 [1024, 768], P('label'), may hold values from -0.0014648438 to 0.0014648438
- tail_second: float32 [1024, 768], P('label'), may hold values from 1e-09 to 2e-07
Outputs:
- feature_grad: bfloat16 [8192, 768], P(('dp', 'label'))
- head_weight_new: float32 [256, 768], P('label')
- head_first_new: float32 [256, 768], P('label')
- head_second_new: float32 [256, 768], P('label')
- tail_weight_new: float32 [1024, 768], P('label')
- tail_first_new: float32 [1024, 768], P('label')
- tail_second_new: float32 [1024, 768], P('label')
The draws below stay inside these ranges and needn't reach their ends.
Inputs may be any that keep to these rules, and one draw needn't show every extreme that they name: `tail_labels`: an instance's 16 tail labels form 2 groups of 8 in a row; the labels of a group are distinct and all lie at one owner (label id // 128), and the 2 owners of an instance differ. For s < counts[b, o], slots[b, o, s] lists without repeats the local indices of the instances of block b that have tail labels at owner o, each such instance exactly once; entries beyond the count are arbitrary local indices. The counts of one block sum to 512; in every block some owner has exactly 128, and the blocks b with equal b // 8 give 128 to the same owner.
All inputs are finite; a program needn't handle non-finite values. No bound on the sum of `tail_positive` on one device may be relied on, other than what follows from the above.
Results may differ from the reference program's by a relative error of at most 0.015.
Values may be sent and summed in bfloat16 or wider, within the bound.
No kernel may reach another device: no remote copies, remote signals or barrier semaphores. Data moves between devices by JAX's collectives and lax.ppermute only.
A program may use at most 64 MiB of HBM per device.

```python
import math
import jax
import jax.numpy as jnp
import numpy as np
from jax import lax

D = 768
TOK_DEV = 256
TAIL_DEV = 128
HP = 4
GROUPS = 2
K = 8
ADAM_STEP = 10
OWNERS = 8
BLOCKS = 32
TOKENS = 8192
HEAD = 256
TAIL = 1024
SHORT = 16
CAP = 128


def routing(key):
    mean_load = TOK_DEV * GROUPS // OWNERS

    def one_block(device):
        device_key = jax.random.fold_in(jax.random.fold_in(key, 11), device)
        row_key = jax.random.fold_in(jax.random.fold_in(key, 13), device // OWNERS)
        hot_owner = jax.random.randint(row_key, (), 0, OWNERS).astype(jnp.int32)
        owner_scores = jax.random.permutation(jax.random.fold_in(device_key, 1), OWNERS).astype(jnp.int32)
        owner_scores = jnp.where(jnp.arange(OWNERS, dtype=jnp.int32) == hot_owner, -1, owner_scores)
        owner_order = jnp.argsort(owner_scores).astype(jnp.int32)
        deltas = jax.random.randint(jax.random.fold_in(device_key, 2), (OWNERS // 2,), -mean_load, mean_load + 1).astype(jnp.int32)
        deltas = deltas.at[0].set(mean_load)
        in_order = jnp.stack([mean_load + deltas, mean_load - deltas], axis=1).reshape(OWNERS).astype(jnp.int32)
        slot_counts = jnp.zeros((OWNERS,), jnp.int32).at[owner_order].set(in_order)
        run_ends = jnp.cumsum(slot_counts).astype(jnp.int32)
        run_starts = run_ends - slot_counts
        shuffle = jax.random.permutation(jax.random.fold_in(device_key, 3), TOK_DEV).astype(jnp.int32)
        positions = (run_starts[:, None] + jnp.arange(CAP, dtype=jnp.int32)[None, :]) % TOK_DEV
        slot_table = shuffle[positions]
        entries = jnp.argsort(shuffle).astype(jnp.int32)[:, None] + TOK_DEV * jnp.arange(GROUPS, dtype=jnp.int32)[None, :]
        owner_of = jnp.sum((run_ends[None, None, :] <= entries[:, :, None]).astype(jnp.int32), axis=2)
        rank_scores = jax.random.randint(jax.random.fold_in(device_key, 4), (TOK_DEV, GROUPS, TAIL_DEV), 0, 65536).astype(jnp.int32) * TAIL_DEV + jnp.arange(TAIL_DEV, dtype=jnp.int32)
        unused_values, row_ids = lax.top_k(rank_scores, K)
        label_ids = (owner_of[:, :, None] * TAIL_DEV + row_ids.astype(jnp.int32)).reshape(TOK_DEV, SHORT)
        return (slot_table.astype(jnp.int32), slot_counts.astype(jnp.int32), label_ids.astype(jnp.int32))
    return lax.map(one_block, jnp.arange(BLOCKS, dtype=jnp.int32))


def draw_slots(key, part):
    return routing(key)[0]


def draw_counts(key, part):
    return routing(key)[1]


def draw_tail_labels(key, part):
    return routing(key)[2].reshape(TOKENS, SHORT)


def touch_ends(values, own_key, least, top_value):
    spot = [jax.random.randint(jax.random.fold_in(own_key, axis), (), 0, length) for axis, length in enumerate(values.shape)]
    widest = values.shape.index(max(values.shape))
    next_to = spot[:widest] + [(spot[widest] + 1) % values.shape[widest]] + spot[widest + 1:]
    return values.at[tuple(spot)].set(least).at[tuple(next_to)].set(top_value)


def levels(key, extent, shards, low, top_value):
    def one(dim, parts):
        steps = jax.random.uniform(jax.random.fold_in(jax.random.fold_in(key, 6), dim), (parts,), jnp.float32, low / len(shards), top_value / len(shards))
        return jnp.repeat(jnp.exp(steps), extent[dim] // parts).reshape((-1,) + (1,) * (len(extent) - dim - 1))

    loudness = one(*shards[0])
    for cut in shards[1:]:
        loudness = loudness * one(*cut)
    return loudness


def cumulative_ranks(amount, lean):
    weights = [(1 << 20) // math.isqrt(grade ** lean) + 1 for grade in range(1, amount + 1)]
    deviation = 1 + sum(weights) // (1 << 30)
    return np.cumsum(np.array([max(1, weight // deviation) for weight in weights]))


def ranked(own_key, shape, count, slope):
    grid = cumulative_ranks(count, slope)
    pick = jax.random.randint(jax.random.fold_in(own_key, 1), shape, 0, int(grid[count - 1]))
    standing = jnp.searchsorted(jnp.asarray(grid, jnp.int32), pick, side="right")
    return jax.random.permutation(jax.random.fold_in(own_key, 2), count)[standing].astype(jnp.int32)


def centred(stream_key, extent, width, most, cuts=(), kind=jnp.bfloat16):
    values = width * jax.random.normal(stream_key, extent, jnp.float32)
    if cuts:
        values = values * levels(stream_key, extent, cuts, -0.22, 0.18)
    return jnp.clip(values, -most, most).astype(kind)


def setup_inputs(seed: int = 0) -> dict:
    keys = jax.random.split(jax.random.key(seed), 13)
    return {
        "features": centred(keys[0], (TOKENS, D), 1.0, 6.0, ((0, 32),)),
        "head_targets": touch_ends(ranked(keys[1], (TOKENS, HP), HEAD, 2), jax.random.fold_in(keys[1], 3), 0, HEAD - 1).astype(jnp.int32),
        "tail_labels": draw_tail_labels(jax.random.fold_in(keys[12], 71), 0),
        "tail_positive": touch_ends((jax.random.randint(keys[3], (TOKENS, SHORT), 0, 4) < 1).astype(jnp.int32), jax.random.fold_in(keys[3], 1), 0, 1),
        "slots": draw_slots(jax.random.fold_in(keys[12], 71), 0),
        "counts": draw_counts(jax.random.fold_in(keys[12], 71), 0),
        "head_weight": centred(keys[6], (HEAD, D), D ** -0.5, 0.21875, ((0, 8),), jnp.float32),
        "head_first": centred(keys[7], (HEAD, D), 0.002, 0.03125, ((0, 8),), jnp.float32),
        "head_second": jnp.clip(jnp.exp(math.log(1.9999999494757503e-05) - 5.2983173 * jax.random.uniform(keys[8], (HEAD, D), jnp.float32) ** levels(keys[8], (HEAD, D), ((0, 8),), -0.2, 0.2)), 1.0000000116860974e-07, 1.9999999494757503e-05),
        "tail_weight": centred(keys[9], (TAIL, D), D ** -0.5, 0.21875, ((0, 8),), jnp.float32),
        "tail_first": centred(keys[10], (TAIL, D), 0.0001, 0.0014648438, ((0, 8),), jnp.float32),
        "tail_second": jnp.clip(jnp.exp(math.log(2.0000000233721948e-07) - 5.2983174 * jax.random.uniform(keys[11], (TAIL, D), jnp.float32) ** levels(keys[11], (TAIL, D), ((0, 8),), -0.2, 0.2)), 9.999999717180685e-10, 2.0000000233721948e-07),
    }


def adam_update(weight, first_moment, second, gradient):
    correct_first = 1.0 - 0.9 ** ADAM_STEP
    correct_second = 1.0 - 0.95 ** ADAM_STEP
    first_new = 0.9 * first_moment + 0.1 * gradient
    second_new = 0.95 * second + 0.05 * gradient * gradient
    weight_new = weight - 0.003 * (first_new / correct_first) / (jnp.sqrt(second_new / correct_second) + 1e-08)
    return (weight_new, first_new, second_new)

def reference(features, head_targets, tail_labels, tail_positive, slots, counts, head_weight, head_first, head_second, tail_weight, tail_first, tail_second):
    head_bf = head_weight.astype(jnp.bfloat16)
    tail_bf = tail_weight.astype(jnp.bfloat16)
    block_count = slots.shape[0]
    feature_blocks = features.reshape(block_count, TOK_DEV, D)
    target_blocks = head_targets.reshape(block_count, TOK_DEV, HP)
    label_blocks = tail_labels.reshape(block_count, TOK_DEV, SHORT)
    positive_blocks = tail_positive.reshape(block_count, TOK_DEV, SHORT)
    head_ids = jnp.arange(HEAD, dtype=jnp.int32)
    owner_ids = jnp.arange(OWNERS, dtype=jnp.int32)

    def one_block(running, inputs):
        head_sum, tail_sum = running
        block_features, targets, labels, positive, slot_ids, slot_count = inputs
        logits = lax.dot_general(block_features, head_bf, (((1,), (1,)), ((), ())), preferred_element_type=jnp.float32)
        is_target = jnp.any(targets[:, :, None] == head_ids[None, None, :], axis=1).astype(jnp.float32)
        head_coef = (jax.nn.sigmoid(logits) - is_target).astype(jnp.bfloat16)
        gradient_rows = jnp.dot(head_coef, head_bf, preferred_element_type=jnp.float32)
        head_sum = head_sum + lax.dot_general(head_coef, block_features, (((0,), (0,)), ((), ())), preferred_element_type=jnp.float32)
        valid_slots = (jnp.arange(CAP, dtype=jnp.int32)[None, :] < slot_count[:, None]).astype(jnp.int32)
        owner_grid = jnp.broadcast_to(owner_ids[:, None], slot_ids.shape)
        presence = jnp.zeros((TOK_DEV, OWNERS), jnp.int32).at[slot_ids, owner_grid].add(valid_slots)
        weight = jnp.take_along_axis(presence, (labels // TAIL_DEV).astype(jnp.int32), axis=1).astype(jnp.float32)
        label_rows = tail_bf[labels]
        tail_logits = jnp.einsum('td,tsd->ts', block_features.astype(jnp.float32), label_rows.astype(jnp.float32), precision=lax.Precision.HIGHEST)
        tail_coef = (weight * (jax.nn.sigmoid(tail_logits) - positive.astype(jnp.float32))).astype(jnp.bfloat16)
        owner_term = jnp.einsum('tgk,tgkd->tgd', tail_coef.reshape(TOK_DEV, GROUPS, K).astype(jnp.float32), label_rows.reshape(TOK_DEV, GROUPS, K, D).astype(jnp.float32), precision=lax.Precision.HIGHEST).astype(jnp.bfloat16)
        gradient_rows = gradient_rows + lax.optimization_barrier(jnp.sum(owner_term.astype(jnp.float32), axis=1))
        update = (tail_coef.astype(jnp.float32)[:, :, None] * block_features.astype(jnp.float32)[:, None, :]).reshape(TOK_DEV * SHORT, D)
        tail_sum = tail_sum.at[labels.reshape(-1)].add(update)
        return ((head_sum, tail_sum), gradient_rows.astype(jnp.bfloat16))
    initial = (jnp.zeros((HEAD, D), jnp.float32), jnp.zeros((TAIL, D), jnp.float32))
    (head_sum, tail_sum), gradient_blocks = lax.scan(one_block, initial, (feature_blocks, target_blocks, label_blocks, positive_blocks, slots, counts))
    feature_grad = gradient_blocks.reshape(TOKENS, D)
    head_new = adam_update(head_weight, head_first, head_second, head_sum / TOKENS)
    tail_new = adam_update(tail_weight, tail_first, tail_second, tail_sum / TOKENS)
    return (feature_grad, head_new[0], head_new[1], head_new[2], tail_new[0], tail_new[1], tail_new[2])
```

```python
import jax
import jax.numpy as jnp
from jax import lax
from jax.sharding import PartitionSpec as P

GROUPS = 2
K = 8
ADAM_STEP = 10


def adam_update(weight, first_moment, second, gradient):
    correct_first = 1.0 - 0.9**ADAM_STEP
    correct_second = 1.0 - 0.95**ADAM_STEP
    first_new = 0.9 * first_moment + 0.1 * gradient
    second_new = 0.95 * second + 0.05 * gradient * gradient
    weight_new = weight - 0.003 * (first_new / correct_first) / (
        jnp.sqrt(second_new / correct_second) + 1e-08
    )
    return (weight_new, first_new, second_new)


def flip(value, axis, bits):
    size = lax.axis_size(axis)
    return lax.ppermute(value, axis, [(i, i ^ bits) for i in range(size)])


def gather_dp(value):
    size = lax.axis_size("dp")
    parts = {0: value}
    bit = size // 2
    while bit:
        parts.update({k | bit: flip(v, "dp", bit) for k, v in list(parts.items())})
        bit //= 2
    return [parts[k] for k in range(size)]


def gather_label(value):
    size = lax.axis_size("label")
    parts = [value] + [flip(value, "label", k) for k in range(2, size, 2)]
    out = []
    for part in parts:
        out += [part, flip(part, "label", 1)]
    return out


def on_device(
    features,
    head_targets,
    tail_labels,
    tail_positive,
    slots,
    counts,
    head_weight,
    head_first,
    head_second,
    tail_weight,
    tail_first,
    tail_second,
):
    tok, width = features.shape
    owners = lax.axis_size("label")
    replicas = lax.axis_size("dp")
    at_dp = lax.axis_index("dp")
    at_label = lax.axis_index("label")
    tail_local = tail_weight.shape[0]
    head_local = head_weight.shape[0]
    token_total = tok * owners * replicas
    f32, bf16 = jnp.float32, jnp.bfloat16
    tq, hq = tail_local // replicas, head_local // replicas
    piece = tq + hq

    own = jnp.concatenate(
        [
            lax.dynamic_slice_in_dim(tail_weight, at_dp * tq, tq),
            lax.dynamic_slice_in_dim(head_weight, at_dp * hq, hq),
        ]
    ).astype(bf16)
    rows = jnp.concatenate(gather_label(own))

    feats = jnp.concatenate(gather_dp(features))

    slot_ids = slots[0]
    slot_width = slot_ids.shape[1]
    valid = jnp.arange(slot_width, dtype=jnp.int32)[None, :] < counts[0][:, None]
    here = jnp.arange(tok, dtype=jnp.int32)[:, None, None]
    presence = jnp.sum(((slot_ids[None] == here) & valid[None]).astype(jnp.int32), axis=2)
    group_owner = tail_labels[:, ::K] // tail_local
    weight = jnp.sum(
        jnp.where(
            group_owner[:, :, None] == jnp.arange(owners, dtype=jnp.int32), presence[:, None, :], 0
        ),
        axis=2,
    )
    info = jnp.concatenate(
        [
            tail_labels // 256,
            tail_labels % 256,
            tail_positive,
            head_targets // 256,
            head_targets % 256,
            weight,
        ],
        axis=1,
    ).astype(bf16)
    info = jnp.concatenate(gather_dp(info)).astype(f32)
    short = tail_labels.shape[1]
    positives = head_targets.shape[1]
    labels = info[:, :short] * 256 + info[:, short : 2 * short]
    pos = info[:, 2 * short : 3 * short]
    at = 3 * short
    targets = info[:, at : at + positives] * 256 + info[:, at + positives : at + 2 * positives]
    weight = info[:, at + 2 * positives :]

    column = jnp.arange(owners * piece, dtype=jnp.int32)
    owner = at_label ^ (column // piece)
    within = column % piece
    is_tail = within < tq
    tail_id = jnp.where(is_tail, owner * tail_local + at_dp * tq + within, -1).astype(f32)[None]
    head_id = jnp.where(is_tail, -1, owner * head_local + at_dp * hq + within - tq).astype(f32)[None]
    base = jnp.where(is_tail, 0.0, 1.0).astype(f32)[None]
    sub = jnp.zeros((1, 1), f32)
    for s in range(short):
        hit = labels[:, s : s + 1] == tail_id
        w = weight[:, s // K : s // K + 1]
        base = base + jnp.where(hit, w, 0.0)
        sub = sub + jnp.where(hit, w * pos[:, s : s + 1], 0.0)
    target = targets[:, 0:1] == head_id
    for s in range(1, positives):
        target = target | (targets[:, s : s + 1] == head_id)
    sub = sub + target.astype(f32)
    base, sub = base.astype(bf16), sub.astype(bf16)

    logits = lax.dot_general(feats, rows, (((1,), (1,)), ((), ())), preferred_element_type=f32)
    coef = (base.astype(f32) * jax.nn.sigmoid(logits) - sub.astype(f32)).astype(bf16)
    grad = lax.dot_general(coef, feats, (((0,), (0,)), ((), ())), preferred_element_type=f32)
    grad = grad.astype(bf16).reshape(owners, piece, width)
    part = jnp.dot(coef, rows, preferred_element_type=f32).astype(bf16)
    part = part.reshape(replicas, tok, width)

    sums = [
        grad[k].astype(f32) + flip(grad[k + 1], "label", 1).astype(f32)
        for k in range(0, owners, 2)
    ]
    total = sums[0]
    for j in range(1, owners // 2):
        total = total + flip(sums[j].astype(bf16), "label", 2 * j).astype(f32)
    total = total.astype(bf16)
    pieces = gather_dp(total)
    stacked = jnp.stack(pieces)
    order = at_dp ^ jnp.arange(replicas, dtype=jnp.int32)
    stacked = stacked[order].astype(f32) / token_total
    tail_gradient = stacked[:, :tq].reshape(tail_local, width)
    head_gradient = stacked[:, tq:].reshape(head_local, width)

    bit = 1
    sums = [part[k] for k in range(replicas)]
    while bit < replicas:
        got = [flip(sums[k + 1], "dp", bit) for k in range(0, len(sums), 2)]
        sums = [sums[2 * j].astype(f32) + got[j].astype(f32) for j in range(len(got))]
        bit *= 2
        if bit < replicas:
            sums = [sums[0]] + [v.astype(bf16) for v in sums[1:]]
    feature_grad = sums[0].astype(bf16)

    head_new = adam_update(head_weight, head_first, head_second, head_gradient)
    tail_new = adam_update(tail_weight, tail_first, tail_second, tail_gradient)
    return (feature_grad, *head_new, *tail_new)


def solution(mesh):
    split = P(("dp", "label"), None)
    rows = P("label", None)
    in_specs = (split,) * 4 + (P(("dp", "label"), None, None), split) + (rows,) * 6
    out_specs = (split,) + (rows,) * 6
    return jax.shard_map(
        on_device, mesh=mesh, in_specs=in_specs, out_specs=out_specs, check_vma=False
    )
```

```python
import functools

import jax
import jax.numpy as jnp
from jax import lax
from jax.experimental import pallas as pl
from jax.experimental.pallas import tpu as pltpu
from jax.sharding import PartitionSpec as P

GROUPS = 2
K = 8
ADAM_STEP = 10


def adam_update(weight, first_moment, second, gradient):
    correct_first = 1.0 - 0.9**ADAM_STEP
    correct_second = 1.0 - 0.95**ADAM_STEP
    first_new = 0.9 * first_moment + 0.1 * gradient
    second_new = 0.95 * second + 0.05 * gradient * gradient
    weight_new = weight - 0.003 * (first_new / correct_first) / (
        jnp.sqrt(second_new / correct_second) + 1e-08
    )
    return (weight_new, first_new, second_new)


def flip(value, axis, bits):
    size = lax.axis_size(axis)
    return lax.ppermute(value, axis, [(i, i ^ bits) for i in range(size)])


def gather_dp(value):
    size = lax.axis_size("dp")
    parts = {0: value}
    bit = size // 2
    while bit:
        for k, v in list(parts.items()):
            parts[k | bit] = flip(v, "dp", bit)
        bit //= 2
    return [parts[k] for k in range(size)]


def gather_label(value):
    size = lax.axis_size("label")
    parts = [value] + [flip(value, "label", k) for k in range(2, size, 2)]
    out = []
    for part in parts:
        out += [part, flip(part, "label", 1)]
    return out


def slot_order(owners):
    far = list(range(owners - 1, 0, -2))
    return far + [k - 1 for k in far]


def index_rows(tail_local, labels_ref, positive_ref, targets_ref, slots_ref, counts, out_ref):
    f32, bf16 = jnp.float32, jnp.bfloat16
    short, tok = labels_ref.shape
    positives = targets_ref.shape[0]
    owners, width = slots_ref.shape
    labels = labels_ref[...]
    here = lax.broadcasted_iota(jnp.int32, (tok, width), 0)
    lane = lax.broadcasted_iota(jnp.int32, (1, width), 1)
    row = lax.broadcasted_iota(jnp.int32, (owners, width), 0)
    presence = jnp.zeros((owners, tok), f32)
    for o in range(owners):
        key = jnp.where(lane < counts[0, o], slots_ref[o : o + 1, :], -1)
        match = jnp.where(here == key, 1.0, 0.0).astype(bf16)
        pick = jnp.where(row == o, 1.0, 0.0).astype(bf16)
        presence += lax.dot_general(
            pick, match, (((1,), (1,)), ((), ())), preferred_element_type=f32
        )
    owner_row = lax.broadcasted_iota(jnp.int32, (owners, tok), 0)
    out_ref[:short, :] = labels
    out_ref[short : 2 * short, :] = positive_ref[...]
    last = jnp.zeros((out_ref.shape[0] - 2 * short, tok), jnp.int32)
    at = lax.broadcasted_iota(jnp.int32, last.shape, 0)
    for h in range(positives):
        last = jnp.where(at == h, targets_ref[h : h + 1, :], last)
    for g in range(GROUPS):
        mine = owner_row == labels[g * K : g * K + 1, :] // tail_local
        weight = jnp.sum(jnp.where(mine, presence, 0.0), axis=0, keepdims=True)
        last = jnp.where(at == positives + g, weight.astype(jnp.int32), last)
    out_ref[2 * short :, :] = last


def prep_kernel(tail_local, tq, hq, cut, *refs):
    sources = refs[:7]
    own_ref, info_ref = refs[7:9]
    buffers, sems = refs[9:16], refs[16]
    at_dp = lax.axis_index("dp")
    views = list(sources)
    if cut:
        views[0] = views[0].at[pl.ds(pl.multiple_of(at_dp * tq, tq), tq), :]
        views[1] = views[1].at[pl.ds(pl.multiple_of(at_dp * hq, hq), hq), :]
    copies = [
        pltpu.make_async_copy(view, buffer, sems.at[i])
        for i, (view, buffer) in enumerate(zip(views, buffers))
    ]
    for copy in copies:
        copy.start()
    for copy in copies:
        copy.wait()
    own_ref[:tq, :] = buffers[0][...].astype(jnp.bfloat16)
    own_ref[tq:, :] = buffers[1][...].astype(jnp.bfloat16)
    index_rows(tail_local, *buffers[2:6], buffers[6], info_ref)


def mask_kernel(short, positives, tail_local, head_local, tq, hq, owners, *refs):
    f32, bf16 = jnp.float32, jnp.bfloat16
    infos, (base_ref, sub_ref) = refs[:-2], refs[-2:]
    tok = infos[0].shape[1]
    at_dp = lax.axis_index("dp")
    at_label = lax.axis_index("label")
    column = lax.broadcasted_iota(jnp.int32, (hq, 128), 0)
    head_row = at_dp * hq + column
    tail_row = at_dp * tq + lax.broadcasted_iota(jnp.int32, (tq, 128), 0)
    piece = tq + hq
    for block, info_ref in enumerate(infos):
        for c in range(0, tok, 128):
            lanes = slice(c, c + 128)
            out = slice(block * tok + c, block * tok + c + 128)
            group_owner, hits, takes = [], [], []
            for g in range(GROUPS):
                first = info_ref[g * K : g * K + 1, lanes]
                owner = first // tail_local
                state = jnp.zeros((tq, 128), jnp.int32)
                for s in range(g * K, (g + 1) * K):
                    within = info_ref[s : s + 1, lanes] - owner * tail_local
                    value = 1 + info_ref[short + s : short + s + 1, lanes]
                    state = jnp.where(tail_row == within, value, state)
                at = 2 * short + positives + g
                weight = info_ref[at : at + 1, lanes].astype(f32)
                group_owner.append(owner)
                hits.append(jnp.where(state > 0, weight, 0.0))
                takes.append(jnp.where(state > 1, weight, 0.0))
            for place, k in enumerate(slot_order(owners)):
                owner = at_label ^ k
                rows = slice(place * piece, place * piece + tq)
                base = jnp.zeros((tq, 128), f32)
                sub = jnp.zeros((tq, 128), f32)
                for g in range(GROUPS):
                    mine = group_owner[g] == owner
                    base = jnp.where(mine, hits[g], base)
                    sub = jnp.where(mine, takes[g], sub)
                base_ref[rows, out] = base.astype(bf16)
                sub_ref[rows, out] = sub.astype(bf16)
                target = jnp.zeros((hq, 128), f32)
                for h in range(positives):
                    at = 2 * short + h
                    within = info_ref[at : at + 1, lanes] - owner * head_local
                    target = jnp.where(within == head_row, 1.0, target)
                rows = slice(place * piece + tq, (place + 1) * piece)
                base_ref[rows, out] = jnp.ones((hq, 128), bf16)
                sub_ref[rows, out] = target.astype(bf16)


def adam_kernel(token_total, tq, hq, *refs):
    states, outs = refs[-12:-6], refs[-6:]
    at_dp = lax.axis_index("dp")
    for k, piece_ref in enumerate(refs[:-12]):
        at = at_dp ^ k
        for first, count, column in ((0, hq, tq), (3, tq, 0)):
            rows = pl.ds(pl.multiple_of(at * count, count), count)
            gradient = piece_ref[column : column + count, :].astype(jnp.float32) / token_total
            new = adam_update(*(ref[rows, :] for ref in states[first : first + 3]), gradient)
            for ref, value in zip(outs[first : first + 3], new):
                ref[rows, :] = value


def in_dp_order(parts):
    at_dp = lax.axis_index("dp")
    size = len(parts)
    bit = 1
    while bit < size:
        odd = (at_dp & bit) != 0
        parts = [jnp.where(odd, parts[k ^ bit], parts[k]) for k in range(size)]
        bit *= 2
    return parts


def on_device(
    features,
    head_targets,
    tail_labels,
    tail_positive,
    slots,
    counts,
    head_weight,
    head_first,
    head_second,
    tail_weight,
    tail_first,
    tail_second,
):
    tok, width = features.shape
    owners = lax.axis_size("label")
    replicas = lax.axis_size("dp")
    at_dp = lax.axis_index("dp")
    tail_local = tail_weight.shape[0]
    head_local = head_weight.shape[0]
    token_total = tok * owners * replicas
    short = tail_labels.shape[1]
    positives = head_targets.shape[1]
    f32, bf16 = jnp.float32, jnp.bfloat16
    tq, hq = tail_local // replicas, head_local // replicas
    piece = tq + hq
    vmem = pl.BlockSpec(memory_space=pltpu.VMEM)

    feats = jnp.concatenate(gather_dp(features))

    info_rows = -(-(2 * short + positives + GROUPS) // 8) * 8
    cut = hq % 8 == 0 and tq % 16 == 0
    share = (tail_weight, head_weight)
    if not cut:
        share = (
            lax.dynamic_slice_in_dim(tail_weight, at_dp * tq, tq),
            lax.dynamic_slice_in_dim(head_weight, at_dp * hq, hq),
        )
    prep = pl.pallas_call(
        functools.partial(prep_kernel, tail_local, tq, hq, cut),
        out_shape=(
            jax.ShapeDtypeStruct((piece, width), bf16),
            jax.ShapeDtypeStruct((info_rows, tok), jnp.int32),
        ),
        in_specs=[pl.BlockSpec(memory_space=pltpu.HBM)] * 7,
        out_specs=(vmem, vmem),
        scratch_shapes=[
            pltpu.VMEM((tq, width), f32),
            pltpu.VMEM((hq, width), f32),
            pltpu.VMEM((short, tok), jnp.int32),
            pltpu.VMEM((short, tok), jnp.int32),
            pltpu.VMEM((positives, tok), jnp.int32),
            pltpu.VMEM(slots.shape[1:], jnp.int32),
            pltpu.SMEM(counts.shape, jnp.int32),
            pltpu.SemaphoreType.DMA((7,)),
        ],
        name="prep",
    )
    own, info = prep(
        *share, tail_labels.T, tail_positive.T, head_targets.T, slots[0], counts
    )
    pieces = gather_label(own)
    rows = jnp.concatenate([pieces[k] for k in slot_order(owners)])
    infos = gather_dp(info)
    masks = jax.ShapeDtypeStruct((owners * piece, replicas * tok), bf16)
    base, sub = pl.pallas_call(
        functools.partial(
            mask_kernel, short, positives, tail_local, head_local, tq, hq, owners
        ),
        out_shape=(masks, masks),
        in_specs=[vmem] * replicas,
        out_specs=(vmem, vmem),
        compiler_params=pltpu.CompilerParams(vmem_limit_bytes=16 << 20),
        name="mask",
    )(*infos)

    logits = lax.dot_general(rows, feats, (((1,), (1,)), ((), ())), preferred_element_type=f32)
    coef = (base.astype(f32) * jax.nn.sigmoid(logits) - sub.astype(f32)).astype(bf16)
    grad = jnp.dot(coef, feats, preferred_element_type=f32).astype(bf16)
    part = lax.dot_general(
        coef, rows, (((0,), (0,)), ((), ())), preferred_element_type=f32
    ).astype(bf16)
    part = part.reshape(replicas, tok, width)

    half = owners // 2 * piece
    cuts = (0, owners // 4 * piece, half)
    sums = []
    for lo, hi in zip(cuts, cuts[1:]):
        got = flip(grad[lo:hi], "label", 1)
        sums.append(grad[half + lo : half + hi].astype(f32) + got.astype(f32))
    sums = jnp.concatenate(sums)
    steps = slot_order(owners)[owners // 2 :]
    total = sums[-piece:]
    for n, k in enumerate(steps[:-1]):
        got = flip(sums[n * piece : (n + 1) * piece].astype(bf16), "label", k)
        total = total + got.astype(f32)
    done = gather_dp(total.astype(bf16))

    bit = 1
    sums = [part[k] for k in range(replicas)]
    while bit < replicas:
        got = [flip(sums[k + 1], "dp", bit) for k in range(0, len(sums), 2)]
        sums = [sums[2 * j].astype(f32) + got[j].astype(f32) for j in range(len(got))]
        bit *= 2
        if bit < replicas:
            sums = [sums[0]] + [v.astype(bf16) for v in sums[1:]]
    feature_grad = sums[0].astype(bf16)

    states = (head_weight, head_first, head_second, tail_weight, tail_first, tail_second)
    if cut:
        new = pl.pallas_call(
            functools.partial(adam_kernel, token_total, tq, hq),
            out_shape=tuple(jax.ShapeDtypeStruct(v.shape, v.dtype) for v in states),
            in_specs=[vmem] * (replicas + 6),
            out_specs=(vmem,) * 6,
            compiler_params=pltpu.CompilerParams(vmem_limit_bytes=12 << 20),
            name="adam",
        )(*done, *states)
    else:
        done = in_dp_order(done)
        tail_gradient = jnp.concatenate([p[:tq] for p in done]).astype(f32) / token_total
        head_gradient = jnp.concatenate([p[tq:] for p in done]).astype(f32) / token_total
        new = adam_update(*states[:3], head_gradient) + adam_update(*states[3:], tail_gradient)
    return (feature_grad, *new)


def solution(mesh):
    split = P(("dp", "label"), None)
    rows = P("label", None)
    in_specs = (split,) * 4 + (P(("dp", "label"), None, None), split) + (rows,) * 6
    out_specs = (split,) + (rows,) * 6
    return jax.shard_map(
        on_device, mesh=mesh, in_specs=in_specs, out_specs=out_specs, check_vma=False
    )
```

```python
import functools

import jax
import jax.numpy as jnp
from jax import lax
from jax.experimental import pallas as pl
from jax.experimental.pallas import tpu as pltpu
from jax.sharding import PartitionSpec as P

GROUPS = 2
K = 8
ADAM_STEP = 10


def adam_update(weight, first_moment, second, gradient):
    correct_first = 1.0 - 0.9**ADAM_STEP
    correct_second = 1.0 - 0.95**ADAM_STEP
    first_new = 0.9 * first_moment + 0.1 * gradient
    second_new = 0.95 * second + 0.05 * gradient * gradient
    weight_new = weight - 0.003 * (first_new / correct_first) / (
        jnp.sqrt(second_new / correct_second) + 1e-08
    )
    return (weight_new, first_new, second_new)


def flip(value, axis, bits):
    size = lax.axis_size(axis)
    return lax.ppermute(value, axis, [(i, i ^ bits) for i in range(size)])


def dp_order(size):
    order, bit = [0], size // 2
    while bit:
        order += [k | bit for k in order]
        bit //= 2
    return order


def gather_dp(value, near=None):
    parts = [value]
    bit = lax.axis_size("dp") // 2
    while bit:
        parts += [flip(v, "dp", bit) for v in parts]
        bit //= 2
    return jnp.concatenate([value if near is None else near] + parts[1:])


def gather_dp_joined(value):
    bit = lax.axis_size("dp") // 2
    while bit:
        value = jnp.concatenate([value, flip(value, "dp", bit)])
        bit //= 2
    return value


def stage_kernel(in_ref, out_ref):
    out_ref[...] = in_ref[...]


def gather_label(value):
    size = lax.axis_size("label")
    parts = [value] + [flip(value, "label", k) for k in range(2, size, 2)]
    out = []
    for part in parts:
        out += [part, flip(part, "label", 1)]
    return out


def slot_order(owners):
    far = list(range(owners - 1, 0, -2))
    return far + [k - 1 for k in far]


def index_lines(short, positives):
    starts, at = [], 0
    for count in (short, short, GROUPS, GROUPS, positives, positives):
        starts.append(at)
        at += count
    return starts, at


def index_values(tail_local, labels_ref, positive_ref, targets_ref, slots_ref, counts):
    f32, bf16 = jnp.float32, jnp.bfloat16
    _, tok = labels_ref.shape
    owners, width = slots_ref.shape
    labels = labels_ref[...]
    here = lax.broadcasted_iota(jnp.int32, (tok, width), 0)
    lane = lax.broadcasted_iota(jnp.int32, (1, width), 1)
    row = lax.broadcasted_iota(jnp.int32, (owners, width), 0)
    presence = jnp.zeros((owners, tok), f32)
    for o in range(owners):
        key = jnp.where(lane < counts[0, o], slots_ref[o : o + 1, :], -1)
        match = jnp.where(here == key, 1.0, 0.0).astype(bf16)
        pick = jnp.where(row == o, 1.0, 0.0).astype(bf16)
        presence += lax.dot_general(
            pick, match, (((1,), (1,)), ((), ())), preferred_element_type=f32
        )
    owner_row = lax.broadcasted_iota(jnp.int32, (owners, tok), 0)
    owner = labels // tail_local
    weights = []
    for g in range(GROUPS):
        mine = owner_row == owner[g * K : g * K + 1, :]
        weights.append(jnp.sum(jnp.where(mine, presence, 0.0), axis=0, keepdims=True))
    targets = targets_ref[...]
    high = targets // 256
    lines = [labels - owner * tail_local, positive_ref[...]]
    lines += [owner[g * K : g * K + 1, :] for g in range(GROUPS)] + weights
    lines += [high, targets - high * 256]
    return [
        line[i : i + 1, :].astype(f32) for line in lines for i in range(line.shape[0])
    ]


def prep_kernel(tail_local, tq, hq, cut, *refs):
    sources = refs[:7]
    own_ref, lines_ref = refs[7:9]
    buffers, sems = refs[9:16], refs[16]
    at_dp = lax.axis_index("dp")
    tok = sources[2].shape[1]
    views = list(sources)
    if cut:
        views[0] = views[0].at[pl.ds(pl.multiple_of(at_dp * tq, tq), tq), :]
        views[1] = views[1].at[pl.ds(pl.multiple_of(at_dp * hq, hq), hq), :]
    copies = [
        pltpu.make_async_copy(view, target, sems.at[i])
        for i, (view, target) in enumerate(zip(views, buffers))
    ]
    for copy in copies:
        copy.start()
    for copy in copies:
        copy.wait()
    own_ref[:tq, :] = buffers[0][...].astype(jnp.bfloat16)
    own_ref[tq:, :] = buffers[1][...].astype(jnp.bfloat16)
    lines = index_values(tail_local, *buffers[2:6], buffers[6])
    count, width = lines_ref.shape
    lines_a_row = width // tok
    at = lax.broadcasted_iota(jnp.int32, (count, tok), 0)
    for lane in range(lines_a_row):
        block = jnp.zeros((count, tok), jnp.float32)
        for row, line in enumerate(lines[lane::lines_a_row]):
            block = jnp.where(at == row, line, block)
        lines_ref[:, lane * tok : (lane + 1) * tok] = block.astype(jnp.bfloat16)


def mask_kernel(short, positives, tq, hq, owners, tok, lines_ref, base_ref, sub_ref):
    f32, bf16 = jnp.float32, jnp.bfloat16
    replicas = base_ref.shape[1] // tok
    count = lines_ref.shape[0] // replicas
    lines_a_row = lines_ref.shape[1] // tok
    starts, _ = index_lines(short, positives)
    at_dp = lax.axis_index("dp")
    at_label = lax.axis_index("label")
    piece = tq + hq
    head_local = hq * replicas
    head_row = (at_dp * hq + lax.broadcasted_iota(jnp.int32, (hq, 128), 0)).astype(f32)
    tail_row = (at_dp * tq + lax.broadcasted_iota(jnp.int32, (tq, 128), 0)).astype(f32)
    for block in range(replicas):
        rows = lines_ref[block * count : (block + 1) * count, :].astype(f32)
        for c in range(0, tok, 128):

            def line(kind, i):
                n = starts[kind] + i
                lane = (n % lines_a_row) * tok + c
                row = n // lines_a_row
                return rows[row : row + 1, lane : lane + 128]

            out = slice(block * tok + c, block * tok + c + 128)
            hits, takes = [], []
            for g in range(GROUPS):
                state = jnp.zeros((tq, 128), f32)
                for s in range(g * K, (g + 1) * K):
                    state = jnp.where(tail_row == line(0, s), 1.0 + line(1, s), state)
                weight = line(3, g)
                hits.append(jnp.where(state > 0.0, weight, 0.0))
                takes.append(jnp.where(state > 1.0, weight, 0.0))
            targets = [256.0 * line(4, h) + line(5, h) for h in range(positives)]
            for place, k in enumerate(slot_order(owners)):
                owner = (at_label ^ k).astype(f32)
                out_rows = slice(place * piece, place * piece + tq)
                base = jnp.zeros((tq, 128), f32)
                sub = jnp.zeros((tq, 128), f32)
                for g in range(GROUPS):
                    mine = line(2, g) == owner
                    base = jnp.where(mine, hits[g], base)
                    sub = jnp.where(mine, takes[g], sub)
                base_ref[out_rows, out] = base.astype(bf16)
                sub_ref[out_rows, out] = sub.astype(bf16)
                target = jnp.zeros((hq, 128), f32)
                for value in targets:
                    target = jnp.where(value - owner * head_local == head_row, 1.0, target)
                out_rows = slice(place * piece + tq, (place + 1) * piece)
                base_ref[out_rows, out] = jnp.ones((hq, 128), bf16)
                sub_ref[out_rows, out] = target.astype(bf16)


def adam_kernel(token_total, tq, hq, replicas, *refs):
    states, outs = refs[-12:-6], refs[-6:]
    at_dp = lax.axis_index("dp")
    pieces = [ref.at[i : i + tq + hq] for ref in refs[:-12] for i in range(0, ref.shape[0], tq + hq)]
    for piece_ref, k in zip(pieces, dp_order(replicas)):
        at = at_dp ^ k
        for first, count, column in ((0, hq, tq), (3, tq, 0)):
            rows = pl.ds(pl.multiple_of(at * count, count), count)
            gradient = piece_ref[column : column + count, :].astype(jnp.float32) / token_total
            new = adam_update(*(ref[rows, :] for ref in states[first : first + 3]), gradient)
            for ref, value in zip(outs[first : first + 3], new):
                ref[rows, :] = value


def in_dp_order(value):
    size = lax.axis_size("dp")
    parts = jnp.split(value, size)
    parts = [parts[dp_order(size).index(k)] for k in range(size)]
    at_dp = lax.axis_index("dp")
    bit = 1
    while bit < size:
        odd = (at_dp & bit) != 0
        parts = [jnp.where(odd, parts[k ^ bit], parts[k]) for k in range(size)]
        bit *= 2
    return parts


def on_device(
    features,
    head_targets,
    tail_labels,
    tail_positive,
    slots,
    counts,
    head_weight,
    head_first,
    head_second,
    tail_weight,
    tail_first,
    tail_second,
):
    tok, width = features.shape
    owners = lax.axis_size("label")
    replicas = lax.axis_size("dp")
    at_dp = lax.axis_index("dp")
    tail_local = tail_weight.shape[0]
    head_local = head_weight.shape[0]
    token_total = tok * owners * replicas
    short = tail_labels.shape[1]
    positives = head_targets.shape[1]
    f32, bf16 = jnp.float32, jnp.bfloat16
    tq, hq = tail_local // replicas, head_local // replicas
    piece = tq + hq
    vmem = pl.BlockSpec(memory_space=pltpu.VMEM)

    lines_a_row = width // tok
    count = -(-index_lines(short, positives)[1] // lines_a_row // 16) * 16
    cut = hq % 8 == 0 and tq % 16 == 0
    share = (tail_weight, head_weight)
    if not cut:
        share = (
            lax.dynamic_slice_in_dim(tail_weight, at_dp * tq, tq),
            lax.dynamic_slice_in_dim(head_weight, at_dp * hq, hq),
        )
    prep = pl.pallas_call(
        functools.partial(prep_kernel, tail_local, tq, hq, cut),
        out_shape=(
            jax.ShapeDtypeStruct((piece, width), bf16),
            jax.ShapeDtypeStruct((count, width), bf16),
        ),
        in_specs=[pl.BlockSpec(memory_space=pltpu.HBM)] * 7,
        out_specs=(vmem, vmem),
        scratch_shapes=[
            pltpu.VMEM((tq, width), f32),
            pltpu.VMEM((hq, width), f32),
            pltpu.VMEM((short, tok), jnp.int32),
            pltpu.VMEM((short, tok), jnp.int32),
            pltpu.VMEM((positives, tok), jnp.int32),
            pltpu.VMEM(slots.shape[1:], jnp.int32),
            pltpu.SMEM(counts.shape, jnp.int32),
            pltpu.SemaphoreType.DMA((7,)),
        ],
        compiler_params=pltpu.CompilerParams(vmem_limit_bytes=4 << 20),
        name="prep",
    )
    sources = (*share, tail_labels.T, tail_positive.T, head_targets.T, slots[0], counts)
    own, mine = prep(
        *(pltpu.with_memory_space_constraint(v, pltpu.HBM) for v in sources)
    )
    pieces = gather_label(own)
    order = slot_order(owners)
    halves = order[: owners // 2], order[owners // 2 :]
    rows_far, rows_near = (jnp.concatenate([pieces[k] for k in half]) for half in halves)

    stage = pl.pallas_call(
        stage_kernel,
        out_shape=jax.ShapeDtypeStruct(features.shape, bf16),
        in_specs=[vmem],
        out_specs=vmem,
        compiler_params=pltpu.CompilerParams(vmem_limit_bytes=4 << 20),
        name="stage",
    )
    near = stage(features)
    feats = gather_dp(features, near)
    lines = gather_dp_joined(mine)
    masks = jax.ShapeDtypeStruct((owners * piece, replicas * tok), bf16)
    masked = pl.pallas_call(
        functools.partial(mask_kernel, short, positives, tq, hq, owners, tok),
        out_shape=(masks, masks),
        in_specs=[vmem],
        out_specs=(vmem, vmem),
        compiler_params=pltpu.CompilerParams(vmem_limit_bytes=16 << 20),
        name="mask",
    )
    base, sub = masked(lines)

    def product(rows, at):
        logits = lax.dot_general(rows, feats, (((1,), (1,)), ((), ())), preferred_element_type=f32)
        own_base, own_sub = (v[at : at + rows.shape[0]].astype(f32) for v in (base, sub))
        coef = (own_base * jax.nn.sigmoid(logits) - own_sub).astype(bf16)
        grad = jnp.dot(coef, feats, preferred_element_type=f32).astype(bf16)
        return coef, grad

    half = owners // 2 * piece
    coef_far, grad_far = product(rows_far, 0)
    rows_near, grad_far = lax.optimization_barrier((rows_near, grad_far))
    coef_near, grad_near = product(rows_near, half)
    coef = jnp.concatenate([coef_far, coef_near])
    rows = jnp.concatenate([rows_far, rows_near])
    cut_at = replicas * tok // 2
    sent = lax.dot_general(
        coef[:, cut_at:], rows, (((0,), (0,)), ((), ())), preferred_element_type=f32
    ).astype(bf16)
    coef, sent = lax.optimization_barrier((coef, sent))
    kept = lax.dot_general(
        coef[:, :cut_at], rows, (((0,), (0,)), ((), ())), preferred_element_type=f32
    ).astype(bf16)
    kept = lax.optimization_barrier(kept)

    cuts = (0, owners // 4 * piece, half)
    sums = []
    for lo, hi in zip(cuts, cuts[1:]):
        got = flip(grad_far[lo:hi], "label", 1)
        if sums:
            got, _ = lax.optimization_barrier((got, sums[0]))
        got = got.astype(f32)
        for at in range(0, hi - lo, piece):
            first = lo + at
            sums.append(grad_near[first : first + piece].astype(f32) + got[at : at + piece])
    total = sums[-1]
    for value, k in zip(sums[:-1], slot_order(owners)[owners // 2 :]):
        total = total + flip(value.astype(bf16), "label", k).astype(f32)
    done = gather_dp_joined(total.astype(bf16))

    bit, part = 1, kept
    while bit < replicas:
        if bit > 1:
            cut_at = part.shape[0] // 2
            part, sent = part[:cut_at], part[cut_at:].astype(bf16)
        got = flip(sent, "dp", bit)
        part = part.astype(f32) + got.astype(f32)
        bit *= 2
    feature_grad = part.astype(bf16)

    states = (head_weight, head_first, head_second, tail_weight, tail_first, tail_second)
    if cut:
        new = pl.pallas_call(
            functools.partial(adam_kernel, token_total, tq, hq, replicas),
            out_shape=tuple(jax.ShapeDtypeStruct(v.shape, v.dtype) for v in states),
            in_specs=[vmem] * 7,
            out_specs=(vmem,) * 6,
            compiler_params=pltpu.CompilerParams(vmem_limit_bytes=12 << 20),
            name="adam",
        )(done, *states)
    else:
        done = in_dp_order(done)
        tail_gradient = jnp.concatenate([p[:tq] for p in done]).astype(f32) / token_total
        head_gradient = jnp.concatenate([p[tq:] for p in done]).astype(f32) / token_total
        new = adam_update(*states[:3], head_gradient) + adam_update(*states[3:], tail_gradient)
    return (feature_grad, *new)


def solution(mesh):
    split = P(("dp", "label"), None)
    rows = P("label", None)
    in_specs = (split,) * 4 + (P(("dp", "label"), None, None), split) + (rows,) * 6
    out_specs = (split,) + (rows,) * 6
    return jax.shard_map(
        on_device, mesh=mesh, in_specs=in_specs, out_specs=out_specs, check_vma=False
    )
```
